512 devices in a mesh: gx: 16 (over y, core), gy: 32 (over x, z).
Axes of the slice: x: 4, y: 8, z: 8, core: 2. Of those that a mesh axis runs over, the one named last changes fastest.
Arguments:
- surface: float32 [6, 16, 32, 16, 544], P(None, 'gx', 'gy'), may hold values from -6 to 6
- mig_ids: int32 [16, 32, 8, 1], P('gx', 'gy'), may hold values from 0 to 15, as said below
- mig_count: int32 [16, 32, 8], P('gx', 'gy'), may hold values from 0 to 1, as said below
- near_source: int32 [16, 32, 8, 16], P('gx', 'gy'), may hold values from 0 to 63, as said below
- near_target: int32 [16, 32, 8, 16], P('gx', 'gy'), may hold values from 0 to 15, as said below
- near_count: int32 [16, 32, 8], P('gx', 'gy'), may hold values from 1 to 16, as said below
Outputs:
- velocity: float32 [3, 16, 32, 24, 544], P(None, 'gx', 'gy')
- positions_next: float32 [3, 16, 32, 24, 544], P(None, 'gx', 'gy')
The draws below stay inside these ranges and needn't reach their ends.
Inputs may be any that keep to these rules, and one draw needn't show every extreme that they name: Within one subdomain the 8 entries of mig_ids are distinct slots; none of them is named by near_source of that subdomain or by near_target lists aimed at it. `mig_count`: in every draw some subdomain receives 1 = 1 migrating cell from each of its eight neighbours. `near_source`: the slot 4 * slot + quarter names a slot of the sending subdomain that its migration lists do not name. `near_target`: A slot of the receiving subdomain that its migration lists do not name. Entries at positions near_count and beyond are padding. Every subdomain either has 16 in all eight directions or at most 4 in each; in every draw at least one subdomain has 16 in all eight.
All inputs are finite; a program needn't handle non-finite values.
Results may differ from the reference program's by a relative error of at most 0.0003.
Values sent between devices are 32-bit elements; how exact they have to be, the bound alone decides.
No kernel may reach another device: no remote copies, remote signals or barrier semaphores. Data moves between devices by JAX's collectives and lax.ppermute only.
A program may use at most 64 MiB of HBM per device.

```python
import jax
import jax.numpy as jnp
from jax import lax

P_SIZE = 544
CELLS = 16
MIG = 1
NEAR = 16
GRID_X = 16
GRID_Y = 32
KEEP = 8


neighbours = ((-1, -1), (-1, 0), (-1, 1), (0, -1), (0, 1), (1, -1), (1, 0), (1, 1))


def slot_orders(key):
    keys = jax.random.split(jax.random.fold_in(key, 7), GRID_X * GRID_Y)
    orders = jax.vmap(lambda one_key: jax.random.permutation(one_key, CELLS))(keys)
    return orders.reshape(GRID_X, GRID_Y, CELLS).astype(jnp.int32)


def draw_mig_ids(key, part):
    orders = slot_orders(key)
    return orders[:, :, :8 * MIG].reshape(GRID_X, GRID_Y, 8, MIG).astype(jnp.int32)


def draw_mig_count(key, part):
    counts = jax.random.randint(jax.random.fold_in(key, 8), (GRID_X, GRID_Y, 8), 0, MIG + 1).astype(jnp.int32)
    row_pick = jax.random.randint(jax.random.fold_in(key, 9), (), 0, GRID_X)
    col_pick = jax.random.randint(jax.random.fold_in(key, 10), (), 0, GRID_Y)
    for k, (step_x, step_y) in enumerate(neighbours):
        counts = counts.at[(row_pick - step_x) % GRID_X, (col_pick - step_y) % GRID_Y, k].set(MIG)
    return counts.astype(jnp.int32)


def draw_near_count(key, part):
    busy = jax.random.randint(jax.random.fold_in(key, 12), (GRID_X, GRID_Y), 0, 4) == 0
    row_pick = jax.random.randint(jax.random.fold_in(key, 16), (), 0, GRID_X)
    col_pick = jax.random.randint(jax.random.fold_in(key, 17), (), 0, GRID_Y)
    busy = busy.at[row_pick, col_pick].set(True)
    light = jax.random.randint(jax.random.fold_in(key, 13), (GRID_X, GRID_Y, 8), 1, NEAR // 4 + 1)
    return jnp.where(busy[:, :, None], NEAR, light).astype(jnp.int32)


def draw_near_source(key, part):
    kept = slot_orders(key)[:, :, 8 * MIG:]
    pick = jax.random.randint(jax.random.fold_in(key, 14), (GRID_X, GRID_Y, 8 * NEAR), 0, KEEP)
    slots = jnp.take_along_axis(kept, pick, axis=2).reshape(GRID_X, GRID_Y, 8, NEAR)
    quarter = jax.random.randint(jax.random.fold_in(key, 15), (GRID_X, GRID_Y, 8, NEAR), 0, 4)
    return (slots * 4 + quarter).astype(jnp.int32)


def draw_near_target(key, part):
    kept = slot_orders(key)[:, :, 8 * MIG:]
    lists = []
    for k, (step_x, step_y) in enumerate(neighbours):
        rolled = jnp.roll(kept, (-step_x, -step_y), axis=(0, 1))
        pick = jax.random.randint(jax.random.fold_in(key, 20 + k), (GRID_X, GRID_Y, NEAR), 0, KEEP)
        lists.append(jnp.take_along_axis(rolled, pick, axis=2))
    return jnp.stack(lists, axis=2).astype(jnp.int32)


def block_scale(stream_key, extent, cuts, least, top_value):
    loudness, own = 1.0, jax.random.fold_in(stream_key, 6)
    for position, blocks in cuts:
        steps = jnp.exp(jax.random.uniform(jax.random.fold_in(own, position), (blocks,), jnp.float32, least / len(cuts), top_value / len(cuts)))
        loudness = loudness * jnp.repeat(steps, extent[position] // blocks).reshape([-1 if axis == position else 1 for axis in range(len(extent))])
    return loudness


def noise(stream_key, extent, deviation, limit, pieces=(), kind=jnp.bfloat16):
    array = jax.random.normal(stream_key, extent, jnp.float32) * deviation
    if len(pieces) > 0:
        array = block_scale(stream_key, extent, pieces, -0.22, 0.18) * array
    return jnp.clip(array, min=-limit, max=limit).astype(kind)


def setup_inputs(seed: int = 0) -> dict:
    seeds = jax.random.split(jax.random.key(seed), 7)
    return {
        "surface": noise(seeds[0], (6, GRID_X, GRID_Y, CELLS, P_SIZE), 1.0, 6.0, ((1, 16), (2, 32)), jnp.float32),
        "mig_ids": draw_mig_ids(jax.random.fold_in(seeds[6], 71), 0),
        "mig_count": draw_mig_count(jax.random.fold_in(seeds[6], 71), 0),
        "near_source": draw_near_source(jax.random.fold_in(seeds[6], 71), 0),
        "near_target": draw_near_target(jax.random.fold_in(seeds[6], 71), 0),
        "near_count": draw_near_count(jax.random.fold_in(seeds[6], 71), 0),
    }


neighbours = ((-1, -1), (-1, 0), (-1, 1), (0, -1), (0, 1), (1, -1), (1, 0), (1, 1))
reg_square = 0.09
kernel_scale = 1.0 / (8.0 * 3.141592653589793)
time_step = 0.1

def stokes(targets, sources, density):
    offset = targets[:, :, None] - sources[:, None, :]
    dist_sq = lax.optimization_barrier(jnp.sum(offset * offset, axis=0))
    shifted = dist_sq + reg_square
    inverse = 1.0 / (shifted * jnp.sqrt(shifted))
    weight = (dist_sq + 2.0 * reg_square) * inverse
    project = lax.optimization_barrier(jnp.sum(offset * density[:, None, :], axis=0)) * inverse
    return lax.optimization_barrier(jnp.sum(weight[None] * density[:, None, :] + project[None] * offset, axis=2)) * kernel_scale

def reference(surface, mig_ids, mig_count, near_source, near_target, near_count):
    grid_rows, grid_cols, cell_total, point_total = (surface.shape[1], surface.shape[2], surface.shape[3], surface.shape[4])
    panel_width = point_total // 4
    slot_iota = jnp.arange(cell_total, dtype=jnp.int32)
    move_iota = jnp.arange(MIG, dtype=jnp.int32)
    pair_iota = jnp.arange(NEAR, dtype=jnp.int32)
    leaving = (mig_ids[..., None] == slot_iota) & (move_iota[:, None] < mig_count[..., None, None])
    own_alive = jnp.logical_not(jnp.any(leaving, axis=(2, 3)))
    incoming = []
    in_alive = []
    for k, (step_x, step_y) in enumerate(neighbours):
        sender_data = jnp.roll(surface, (step_x, step_y), axis=(1, 2))
        slots_sent = jnp.roll(mig_ids[:, :, k], (step_x, step_y), axis=(0, 1))
        count_sent = jnp.roll(mig_count[:, :, k], (step_x, step_y), axis=(0, 1))
        select = (slots_sent[..., None] == slot_iota).astype(jnp.float32)
        incoming.append(jnp.einsum('abmc,kabcp->kabmp', select, sender_data, precision=lax.Precision.HIGHEST))
        in_alive.append(move_iota < count_sent[..., None])
    buffer = jnp.concatenate([surface] + incoming, axis=3)
    alive = jnp.concatenate([own_alive] + in_alive, axis=2).astype(jnp.float32)
    slot_total = buffer.shape[3]
    flat_cells = jnp.moveaxis(buffer, 0, 3).reshape(-1, 6, point_total)
    self_flat = lax.map(lambda cell: stokes(cell[:3], cell[:3], cell[3:]), flat_cells)
    self_vel = jnp.moveaxis(self_flat.reshape(grid_rows, grid_cols, slot_total, 3, point_total), 3, 0)
    own_pos = jnp.moveaxis(surface[:3].reshape(3, grid_rows * grid_cols, cell_total, point_total), 1, 0)
    panels_all = surface.reshape(6, grid_rows, grid_cols, cell_total * 4, panel_width)
    near_acc = jnp.zeros((3, grid_rows, grid_cols, cell_total, point_total), jnp.float32)
    for k, (step_x, step_y) in enumerate(neighbours):
        sent_panels = jnp.roll(panels_all, (step_x, step_y), axis=(1, 2))
        sent_panels = jnp.moveaxis(sent_panels.reshape(6, grid_rows * grid_cols, cell_total * 4, panel_width), 1, 0)
        from_ids = jnp.roll(near_source[:, :, k], (step_x, step_y), axis=(0, 1)).reshape(-1, NEAR)
        into_ids = jnp.roll(near_target[:, :, k], (step_x, step_y), axis=(0, 1)).reshape(-1, NEAR)
        pair_used = jnp.roll(near_count[:, :, k], (step_x, step_y), axis=(0, 1)).reshape(-1)

        def receiver(block_args):
            positions, panels, from_one, into_one, used_one = block_args
            panel_set = panels[:, from_one]
            target_pos = positions[:, into_one]
            terms = jax.vmap(stokes, in_axes=(1, 1, 1))(target_pos, panel_set[:3], panel_set[3:])
            mask = (pair_iota < used_one).astype(jnp.float32)
            one_hot = (into_one[:, None] == slot_iota).astype(jnp.float32) * mask[:, None]
            return jnp.einsum('nk,ncp->ckp', one_hot, terms, precision=lax.Precision.HIGHEST)
        summed = lax.map(receiver, (own_pos, sent_panels, from_ids, into_ids, pair_used))
        near_acc = near_acc + jnp.moveaxis(summed, 0, 1).reshape(3, grid_rows, grid_cols, cell_total, point_total)
    padding = jnp.zeros((3, grid_rows, grid_cols, slot_total - cell_total, point_total), jnp.float32)
    near_vel = jnp.concatenate([near_acc, padding], axis=3)
    velocity = alive[None, :, :, :, None] * (self_vel + near_vel)
    positions_next = alive[None, :, :, :, None] * (buffer[:3] + time_step * velocity)
    return (velocity, positions_next)
```

```python
import functools

import jax
import jax.numpy as jnp
from jax import lax
from jax.experimental import pallas as pl
from jax.experimental.pallas import tpu as pltpu
from jax.sharding import PartitionSpec as P

neighbours = ((-1, -1), (-1, 0), (-1, 1), (0, -1), (0, 1), (1, -1), (1, 0), (1, 1))
reg_square = 0.09
kernel_scale = 1.0 / (8.0 * 3.141592653589793)
time_step = 0.1

f32 = jnp.float32
bf16 = jnp.bfloat16
i32 = jnp.int32

CELLS = 16
POINTS = 544
WIDE = 640
PANEL = 136
PANEL_ROWS = 144
KEPT = 8
NEAR = 16
COUNT_AT = 2 * NEAR
MOVES_AT = 2 * NEAR + 1
IDS_AT = 2 * NEAR + 2
SELF_CHUNKS = ((0, 640),)
NEAR_CHUNKS = ((0, 256), (256, 512), (512, 640))

VMEM = pl.BlockSpec(memory_space=pltpu.VMEM)
SMEM = pl.BlockSpec(memory_space=pltpu.SMEM)


def from_behind(value, axis, by):
    size = lax.axis_size(axis)
    return lax.ppermute(value, axis, [(i, (i + by) % size) for i in range(size)])


def split3(value):
    high = value.astype(bf16).astype(f32)
    rest = value - high
    middle = rest.astype(bf16).astype(f32)
    return high, middle, rest - middle


def prepare(part, source_ref, feature_ref, target_ref=None):
    for col in range(source_ref.shape[0]):
        lanes = slice(128 * col, 128 * col + 128)
        pos = [part(a, lanes) for a in range(3)]
        den = [part(3 + a, lanes) for a in range(3)]
        norm = pos[0] * pos[0] + pos[1] * pos[1] + pos[2] * pos[2]
        dot = pos[0] * den[0] + pos[1] * den[1] + pos[2] * den[2]
        pieces = [split3(p) for p in pos]
        one = jnp.ones_like(norm)
        rows = [pieces[a][p] for p in (0, 1, 0, 1, 2, 0) for a in range(3)]
        rows += [*split3(norm + reg_square), one, one, one]
        for i, row in enumerate(rows):
            source_ref[col, 8 * i : 8 * i + 8, :] = row
        if target_ref is not None:
            rows = [-2.0 * pieces[a][p] for p in (0, 0, 1, 1, 0, 2) for a in range(3)]
            rows += [one, one, one, *split3(norm)]
            for i, row in enumerate(rows):
                target_ref[col, 8 * i : 8 * i + 8, :] = row
        found = [*den]
        found += [pos[a] * den[b] for a in range(3) for b in range(3)]
        found += [norm * den[b] + dot * pos[b] for b in range(3)]
        for f, value in enumerate(found):
            for p, piece in enumerate(split3(value)):
                row = 8 * (16 * p + f)
                feature_ref[col, row : row + 8, :] = piece


def clear_padding(source_ref, feature_ref, target_ref=None):
    for col in range(source_ref.shape[0]):
        for ref in (source_ref, target_ref):
            if ref is not None:
                ref[col, 8 * 24 : 8 * 32, :] = jnp.zeros((64, 128), f32)
        for p in range(3):
            row = 8 * (16 * p + 15)
            feature_ref[col, row : row + 8, :] = jnp.zeros((8, 128), f32)


def rows_of(ref, c, rows):
    cols = range(ref.shape[0])
    return jnp.concatenate([ref[col, pl.ds(c, rows, stride=8), :] for col in cols], 1)


def weights(shifted):
    inverse = lax.rsqrt(shifted)
    weight = inverse * inverse * inverse
    high = weight.astype(bf16)
    return high, (weight - high.astype(f32)).astype(bf16)


def main_sums(factors, source, target):
    high, low = weights(jnp.dot(source, target, preferred_element_type=f32))
    first = jnp.dot(factors, high, preferred_element_type=f32)
    second = jnp.dot(factors[0:32], low, preferred_element_type=f32)
    return (first[0:16] + second[0:16]) + ((first[16:32] + second[16:32]) + first[32:48])


def self_terms(c, source_ref, feature_ref, target_ref):
    source = rows_of(source_ref, c, 32)
    factors = rows_of(feature_ref, c, 48).astype(bf16)
    target = rows_of(target_ref, c, 32).astype(bf16)
    rows = source.T.astype(bf16)[0:POINTS]
    found = [
        main_sums(factors[:, 0:POINTS], rows, target[:, start:stop]) for start, stop in SELF_CHUNKS
    ]
    return jnp.concatenate(found, 1), target


def leaving_mask(list_ref):
    mask = jnp.int32(0)
    for k in range(8):
        bit = jnp.int32(1) << list_ref[k, IDS_AT]
        mask = mask | jnp.where(list_ref[k, MOVES_AT] > 0, bit, jnp.int32(0))
    return mask


def pack_kernel(
    ids_hbm, moves_hbm, source_hbm, target_hbm, count_hbm, own_hbm,
    table_ref, right_ref, left_ref, side_ref,
    ids_ref, moves_ref, source_ref, target_ref, count_ref, own_ref, map_ref, sems,
):
    copies = [
        pltpu.make_async_copy(here, there, sems.at[n])
        for n, (here, there) in enumerate(
            (
                (own_hbm, own_ref),
                (ids_hbm, ids_ref),
                (moves_hbm, moves_ref),
                (count_hbm, count_ref),
                (source_hbm, source_ref),
                (target_hbm, target_ref),
            )
        )
    ]
    for copy in copies:
        copy.start()
    for ref in (right_ref, left_ref, side_ref):
        ref[...] = jnp.zeros(ref.shape, f32)
    table_ref[...] = jnp.zeros((8, 128), i32)
    for copy in copies[1:]:
        copy.wait()
    table_ref[:, 0:NEAR] = source_ref[0, 0]
    table_ref[:, NEAR : 2 * NEAR] = target_ref[0, 0]
    lists = table_ref[...]
    row = lax.broadcasted_iota(i32, (8, 128), 0)
    lane = lax.broadcasted_iota(i32, (8, 128), 1)
    used = jnp.int32(0)
    for k in range(8):
        used = used | (jnp.int32(1) << ids_ref[0, 0, k])
        for column, value in (
            (COUNT_AT, count_ref[0, 0, k]),
            (MOVES_AT, moves_ref[0, 0, k]),
            (IDS_AT, ids_ref[0, 0, k]),
        ):
            lists = jnp.where((row == k) & (lane == column), value, lists)
    table_ref[...] = lists
    rank = jnp.int32(0)
    slot = lists >> 2
    ranked = jnp.zeros((8, 128), i32)
    for s in range(CELLS):
        map_ref[s] = jnp.int32(0)
    for s in range(CELLS):
        keep = ((used >> s) & 1) == 0
        ranked = jnp.where(slot == s, rank, ranked)
        map_ref[jnp.where(keep, rank, CELLS - 1)] = jnp.int32(s)
        rank = jnp.where(keep & (rank < KEPT - 1), rank + 1, rank)
    sent = jnp.where(lane < NEAR, ranked * 4 + (lists & 3), lists).astype(f32)
    copies[0].wait()
    for r in range(KEPT):
        s = map_ref[r]
        for a in range(6):
            points = own_ref[a, pl.ds(s, 1), :]
            right_ref[8 * a + r : 8 * a + r + 1, 0:POINTS] = points
            left_ref[8 * a + r : 8 * a + r + 1, 0:POINTS] = points
    for k, ref, base in (
        (2, right_ref, 48), (4, right_ref, 56), (7, right_ref, 64),
        (0, left_ref, 48), (3, left_ref, 56), (5, left_ref, 64),
        (6, side_ref, 0), (1, side_ref, 8),
    ):
        s = ids_ref[0, 0, k]
        for a in range(6):
            ref[base + a : base + a + 1, 0:POINTS] = own_ref[a, pl.ds(s, 1), :]
        ref[base + 6 : base + 7, 0:128] = sent[k : k + 1]


def pack(ids, moves, source, target, count, own):
    wide = jax.ShapeDtypeStruct((72, WIDE), f32)
    return pl.pallas_call(
        pack_kernel,
        out_shape=(
            jax.ShapeDtypeStruct((8, 128), i32), wide, wide, jax.ShapeDtypeStruct((16, WIDE), f32)
        ),
        in_specs=[pl.BlockSpec(memory_space=pl.ANY)] * 6,
        out_specs=(VMEM,) * 4,
        scratch_shapes=[
            pltpu.SMEM(ids.shape, i32),
            pltpu.SMEM(moves.shape, i32),
            pltpu.VMEM(source.shape, i32),
            pltpu.VMEM(target.shape, i32),
            pltpu.SMEM(count.shape, i32),
            pltpu.VMEM(own.shape, f32),
            pltpu.SMEM((CELLS,), i32),
            pltpu.SemaphoreType.DMA((6,)),
        ],
        name="pack",
    )(ids, moves, source, target, count, own)


def join_kernel(right_ref, side_ref, low_ref, high_ref, up_ref, down_ref):
    for ref, side, place in ((up_ref, 0, 64), (down_ref, 8, 48)):
        ref[0:48] = right_ref[0:48]
        ref[48:56] = side_ref[side : side + 8]
        ref[56:104] = low_ref[0:48]
        ref[104:112] = low_ref[place : place + 8]
        ref[112:160] = high_ref[0:48]
        ref[160:168] = high_ref[place : place + 8]


def join(right, side, low, high):
    wide = jax.ShapeDtypeStruct((168, WIDE), f32)
    return pl.pallas_call(
        join_kernel,
        out_shape=(wide, wide),
        in_specs=[VMEM] * 4,
        out_specs=(VMEM, VMEM),
        compiler_params=pltpu.CompilerParams(vmem_limit_bytes=8 << 20),
        name="join",
    )(right, side, low, high)


def own_kernel(
    half, list_ref, own_ref, after_ref, sums_ref, main_ref,
    part_ref, source_ref, feature_ref, target_ref,
):
    leaving = leaving_mask(list_ref)
    part_ref[:, :, WIDE - 128 : WIDE] = jnp.zeros((6, 8, 128), f32)
    for a in range(6):
        part_ref[a, :, 0:POINTS] = own_ref[a, 8 * half : 8 * half + 8, :]
    clear_padding(source_ref, feature_ref, target_ref)
    prepare(lambda a, lanes: part_ref[a, :, lanes], source_ref, feature_ref, target_ref)

    def one_slot(c, carry):
        @pl.when(((leaving >> (c + 8 * half)) & 1) == 0)
        def _():
            sums_ref[c], main_ref[c] = self_terms(c, source_ref, feature_ref, target_ref)

        return carry

    lax.fori_loop(0, 8, one_slot, 0)


def own_sums(table, own, after, half):
    return pl.pallas_call(
        functools.partial(own_kernel, half),
        out_shape=(
            jax.ShapeDtypeStruct((8, 16, WIDE), f32),
            jax.ShapeDtypeStruct((8, 32, WIDE), bf16),
        ),
        in_specs=[SMEM, VMEM, pl.BlockSpec(memory_space=pl.ANY)],
        out_specs=(VMEM, VMEM),
        scratch_shapes=[
            pltpu.VMEM((6, 8, WIDE), f32),
            pltpu.VMEM((5, 256, 128), f32),
            pltpu.VMEM((5, 384, 128), f32),
            pltpu.VMEM((5, 256, 128), f32),
        ],
        compiler_params=pltpu.CompilerParams(vmem_limit_bytes=24 << 20),
        cost_estimate=pl.CostEstimate(flops=8_000_000_000, bytes_accessed=1 << 20, transcendentals=0),
        name=f"own{half}",
    )(table, own, after)


def last_kernel(
    table_ref, own_ref, low_ref, high_ref, up_ref, down_ref,
    sums_a, sums_b, main_a, main_b,
    vel_ref, pos_ref,
    quarter_ref, sums_ref, number_ref, list_ref, moved_ref, part_ref,
    near_source, near_feature, self_source, self_feature, self_target, main_ref, sem,
):
    lane = lax.broadcasted_iota(i32, (8, 256), 1)

    def set_main(slot, value, add=False):
        rows = pl.ds(pl.multiple_of(slot * 16, 16), 16)
        for col in range(WIDE // 128):
            piece = value[:, 128 * col : 128 * col + 128]
            sums_ref[col, rows, :] = sums_ref[col, rows, :] + piece if add else piece

    for k, source, base, start in (
        (4, low_ref, 0, 56), (3, high_ref, 0, 56),
        (6, up_ref, 0, 48), (7, up_ref, 56, 104), (5, up_ref, 112, 160),
        (1, down_ref, 0, 48), (2, down_ref, 56, 104), (0, down_ref, 112, 160),
    ):
        block = source[start : start + 8]
        number_ref[k : k + 1, :] = block[6:7, 0:128].astype(i32)
        for a in range(6):
            moved_ref[a, k : k + 1, :] = block[a : a + 1]
            rows = source[base + 8 * a : base + 8 * a + 8]
            for q in range(4):
                turned = rows if q == 0 else pltpu.roll(rows, WIDE - PANEL * q, 1)
                quarter_ref[k, q, 8 * a : 8 * a + 8] = jnp.where(lane < PANEL, turned[:, 0:256], 0.0)
    copy = pltpu.make_async_copy(number_ref, list_ref, sem)
    copy.start()
    for c in range(8):
        set_main(c, sums_a[c])
        set_main(8 + c, sums_b[c])
    main_ref[0:8] = main_a[...]
    main_ref[8:16] = main_b[...]
    clear_padding(near_source, near_feature)
    clear_padding(self_source, self_feature, self_target)
    prepare(lambda a, lanes: moved_ref[a, :, lanes], self_source, self_feature, self_target)
    leaving = leaving_mask(table_ref)
    copy.wait()

    def one_move(k, carry):
        @pl.when(list_ref[k, MOVES_AT] > 0)
        def _():
            sums, _ = self_terms(k, self_source, self_feature, self_target)
            set_main(CELLS + k, sums)

        return carry

    lax.fori_loop(0, 8, one_move, 0)

    def one_direction(k, carry):
        total = list_ref[k, COUNT_AT]

        def entries(g, which):
            found = []
            for e in which:
                at = jnp.minimum(g * 8 + e, total - 1)
                into = list_ref[k, NEAR + at]
                source = rows_of(near_source, e, 32)
                factors = rows_of(near_feature, e, 48).astype(bf16)
                rows = source.T.astype(bf16)[0:PANEL_ROWS]
                main = [
                    main_sums(factors[:, 0:PANEL_ROWS], rows, main_ref[into, :, start:stop])
                    for start, stop in NEAR_CHUNKS
                ]
                found.append((into, main))
            for into, main in found:
                set_main(into, jnp.concatenate(main, 1), True)

        def one_group(g, inner):
            for e in range(8):
                n = g * 8 + e
                live = jnp.where(n < total, 1.0, 0.0)
                panel = list_ref[k, jnp.minimum(n, total - 1)]
                for a in range(6):
                    row = quarter_ref[k, panel & 3, pl.ds(8 * a + (panel >> 2), 1), :]
                    part_ref[a, e : e + 1, :] = row if a < 3 else row * live
            prepare(lambda a, lanes: part_ref[a, :, lanes], near_source, near_feature)

            @pl.when(g * 8 + 4 < total)
            def _():
                entries(g, range(8))

            @pl.when(g * 8 + 4 >= total)
            def _():
                entries(g, range(4))

            return inner

        lax.fori_loop(0, (total + 7) // 8, one_group, 0)
        return carry

    lax.fori_loop(0, 8, one_direction, 0)

    row = lax.broadcasted_iota(i32, (8, 128), 0)
    for h in range(3):
        alive = jnp.zeros((8, 128), i32)
        for c in range(8):
            here = 1 - ((leaving >> (8 * h + c)) & 1) if h < 2 else jnp.where(list_ref[c, MOVES_AT] > 0, 1, 0)
            alive = jnp.where(row == c, here, alive)
        for start in range(0, WIDE, 128):
            stop = min(start + 128, POINTS)
            lanes = slice(start, stop)
            living = alive[:, 0 : stop - start] > 0
            x = [own_ref[a, 8 * h : 8 * h + 8, lanes] if h < 2 else moved_ref[a, :, lanes] for a in range(3)]
            sums = [sums_ref[start // 128, pl.ds(128 * h + f, 8, stride=16), :][:, 0 : stop - start] for f in range(15)]
            p = sums[0:3]
            r = [sums[3 + 3 * a : 6 + 3 * a] for a in range(3)]
            norm = x[0] * x[0] + x[1] * x[1] + x[2] * x[2] + 2.0 * reg_square
            inner = x[0] * p[0] + x[1] * p[1] + x[2] * p[2] - (r[0][0] + r[1][1] + r[2][2])
            for b in range(3):
                u = norm * p[b] + x[b] * inner + sums[12 + b]
                for a in range(3):
                    u = u - x[a] * (2.0 * r[a][b] + r[b][a])
                u = u * kernel_scale
                vel_ref[b, 8 * h : 8 * h + 8, lanes] = jnp.where(living, u, 0.0)
                pos_ref[b, 8 * h : 8 * h + 8, lanes] = jnp.where(living, x[b] + time_step * u, 0.0)


def last(table, own, low, high, up, down, first, second):
    out = jax.ShapeDtypeStruct((3, CELLS + 8, POINTS), f32)
    both = [value for pair in zip(first, second) for value in pair]
    return pl.pallas_call(
        last_kernel,
        out_shape=(out, out),
        in_specs=[SMEM] + [VMEM] * 9,
        out_specs=(VMEM, VMEM),
        scratch_shapes=[
            pltpu.VMEM((8, 4, 48, 256), f32),
            pltpu.VMEM((5, (CELLS + 8) * 16, 128), f32),
            pltpu.VMEM((8, 128), i32),
            pltpu.SMEM((8, 128), i32),
            pltpu.VMEM((6, 8, WIDE), f32),
            pltpu.VMEM((6, 8, 256), f32),
            pltpu.VMEM((2, 256, 128), f32),
            pltpu.VMEM((2, 384, 128), f32),
            pltpu.VMEM((5, 256, 128), f32),
            pltpu.VMEM((5, 384, 128), f32),
            pltpu.VMEM((5, 256, 128), f32),
            pltpu.VMEM((CELLS, 32, WIDE), bf16),
            pltpu.SemaphoreType.DMA,
        ],
        compiler_params=pltpu.CompilerParams(vmem_limit_bytes=32 << 20),
        cost_estimate=pl.CostEstimate(flops=40_000_000_000, bytes_accessed=1 << 20, transcendentals=0),
        name="last",
    )(table, own, low, high, up, down, *both)


def on_device(surface, mig_ids, mig_count, near_source, near_target, near_count):
    own = surface[:, 0, 0]
    table, right, left, side = pack(mig_ids[:, :, :, 0], mig_count, near_source, near_target, near_count, own)
    low = from_behind(right, "gy", 1)
    high = from_behind(left, "gy", -1)
    first = own_sums(table, own, right, 0)
    to_up, to_down = join(right, side, low, high)
    up = from_behind(to_up, "gx", 1)
    down = from_behind(to_down, "gx", -1)
    second = own_sums(table, own, to_up, 1)
    vel, pos = last(table, own, low, high, up, down, first, second)
    return vel[:, None, None], pos[:, None, None]


def solution(mesh):
    placed = (
        P(None, "gx", "gy", None, None),
        P("gx", "gy", None, None),
        P("gx", "gy", None),
        P("gx", "gy", None, None),
        P("gx", "gy", None, None),
        P("gx", "gy", None),
    )
    return jax.shard_map(
        on_device,
        mesh=mesh,
        in_specs=placed,
        out_specs=(P(None, "gx", "gy", None, None), P(None, "gx", "gy", None, None)),
        check_vma=False,
    )
```

```python
import functools

import jax
import jax.numpy as jnp
from jax import lax
from jax.experimental import pallas as pl
from jax.experimental.pallas import tpu as pltpu
from jax.sharding import PartitionSpec as P

neighbours = ((-1, -1), (-1, 0), (-1, 1), (0, -1), (0, 1), (1, -1), (1, 0), (1, 1))
reg_square = 0.09
kernel_scale = 1.0 / (8.0 * 3.141592653589793)
time_step = 0.1

f32 = jnp.float32
bf16 = jnp.bfloat16
i32 = jnp.int32

CELLS = 16
POINTS = 544
WIDE = 640
PANEL = 136
PANEL_ROWS = 144
KEPT = 8
NEAR = 16
COUNT_AT = 2 * NEAR
MOVES_AT = 2 * NEAR + 1
IDS_AT = 2 * NEAR + 2
SELF_CHUNKS = ((0, 640),)
NEAR_CHUNKS = ((0, 256), (256, 512), (512, 640))

VMEM = pl.BlockSpec(memory_space=pltpu.VMEM)
SMEM = pl.BlockSpec(memory_space=pltpu.SMEM)


def swap(value, axis, odd):
    size = lax.axis_size(axis)
    return lax.ppermute(value, axis, [(i, (((i + odd) ^ 1) - odd) % size) for i in range(size)])


def parity(axis):
    return lax.axis_index(axis) & 1


def split3(value):
    high = value.astype(bf16).astype(f32)
    rest = value - high
    middle = rest.astype(bf16).astype(f32)
    return high, middle, rest - middle


def prepare(part, source_ref, feature_ref, target_ref=None):
    for col in range(source_ref.shape[0]):
        lanes = slice(128 * col, 128 * col + 128)
        pos = [part(a, lanes) for a in range(3)]
        den = [part(3 + a, lanes) for a in range(3)]
        norm = pos[0] * pos[0] + pos[1] * pos[1] + pos[2] * pos[2]
        dot = pos[0] * den[0] + pos[1] * den[1] + pos[2] * den[2]
        pieces = [split3(p) for p in pos]
        one = jnp.ones_like(norm)
        rows = [pieces[a][p] for p in (0, 1, 0, 1, 2, 0) for a in range(3)]
        rows += [*split3(norm + reg_square), one, one, one]
        for i, row in enumerate(rows):
            source_ref[col, 8 * i : 8 * i + 8, :] = row
        if target_ref is not None:
            rows = [-2.0 * pieces[a][p] for p in (0, 0, 1, 1, 0, 2) for a in range(3)]
            rows += [one, one, one, *split3(norm)]
            for i, row in enumerate(rows):
                target_ref[col, 8 * i : 8 * i + 8, :] = row
        found = [*den]
        found += [pos[a] * den[b] for a in range(3) for b in range(3)]
        found += [norm * den[b] + dot * pos[b] for b in range(3)]
        for f, value in enumerate(found):
            for p, piece in enumerate(split3(value)):
                row = 8 * (16 * p + f)
                feature_ref[col, row : row + 8, :] = piece


def clear_padding(source_ref, feature_ref, target_ref=None):
    for col in range(source_ref.shape[0]):
        for ref in (source_ref, target_ref):
            if ref is not None:
                ref[col, 8 * 24 : 8 * 32, :] = jnp.zeros((64, 128), f32)
        for p in range(3):
            row = 8 * (16 * p + 15)
            feature_ref[col, row : row + 8, :] = jnp.zeros((8, 128), f32)


def rows_of(ref, c, rows):
    cols = range(ref.shape[0])
    return jnp.concatenate([ref[col, pl.ds(c, rows, stride=8), :] for col in cols], 1)


def weights(shifted):
    inverse = lax.rsqrt(shifted)
    weight = inverse * inverse * inverse
    high = weight.astype(bf16)
    return high, (weight - high.astype(f32)).astype(bf16)


def main_sums(factors, source, target):
    high, low = weights(jnp.dot(source, target, preferred_element_type=f32))
    first = jnp.dot(factors, high, preferred_element_type=f32)
    second = jnp.dot(factors[0:32], low, preferred_element_type=f32)
    return (first[0:16] + second[0:16]) + ((first[16:32] + second[16:32]) + first[32:48])


def self_terms(c, source_ref, feature_ref, target_ref):
    source = rows_of(source_ref, c, 32)
    factors = rows_of(feature_ref, c, 48).astype(bf16)
    target = rows_of(target_ref, c, 32).astype(bf16)
    rows = source.T.astype(bf16)[0:POINTS]
    found = [
        main_sums(factors[:, 0:POINTS], rows, target[:, start:stop]) for start, stop in SELF_CHUNKS
    ]
    return jnp.concatenate(found, 1), target


def leaving_mask(list_ref):
    mask = jnp.int32(0)
    for k in range(8):
        bit = jnp.int32(1) << list_ref[k, IDS_AT]
        mask = mask | jnp.where(list_ref[k, MOVES_AT] > 0, bit, jnp.int32(0))
    return mask


def pack_kernel(
    ids_hbm, moves_hbm, source_hbm, target_hbm, count_hbm, own_hbm,
    table_ref, even_ref, odd_ref, side_ref,
    sent_ref, ids_ref, moves_ref, source_ref, target_ref, count_ref, own_ref, map_ref, sems,
):
    copies = [
        pltpu.make_async_copy(here, there, sems.at[n])
        for n, (here, there) in enumerate(
            (
                (own_hbm, own_ref),
                (ids_hbm, ids_ref),
                (moves_hbm, moves_ref),
                (count_hbm, count_ref),
                (source_hbm, source_ref),
                (target_hbm, target_ref),
            )
        )
    ]
    for copy in copies:
        copy.start()
    for ref in (even_ref, odd_ref, side_ref):
        ref[...] = jnp.zeros(ref.shape, f32)
    table_ref[...] = jnp.zeros((8, 128), i32)
    for copy in copies[1:]:
        copy.wait()
    table_ref[:, 0:NEAR] = source_ref[0, 0]
    table_ref[:, NEAR : 2 * NEAR] = target_ref[0, 0]
    lists = table_ref[...]
    row = lax.broadcasted_iota(i32, (8, 128), 0)
    lane = lax.broadcasted_iota(i32, (8, 128), 1)
    used = jnp.int32(0)
    for k in range(8):
        used = used | (jnp.int32(1) << ids_ref[0, 0, k])
        for column, value in (
            (COUNT_AT, count_ref[0, 0, k]),
            (MOVES_AT, moves_ref[0, 0, k]),
            (IDS_AT, ids_ref[0, 0, k]),
        ):
            lists = jnp.where((row == k) & (lane == column), value, lists)
    table_ref[...] = lists
    rank = jnp.int32(0)
    slot = lists >> 2
    ranked = jnp.zeros((8, 128), i32)
    for s in range(CELLS):
        map_ref[s] = jnp.int32(0)
    for s in range(CELLS):
        keep = ((used >> s) & 1) == 0
        ranked = jnp.where(slot == s, rank, ranked)
        map_ref[jnp.where(keep, rank, CELLS - 1)] = jnp.int32(s)
        rank = jnp.where(keep & (rank < KEPT - 1), rank + 1, rank)
    sent = jnp.where(lane < NEAR, ranked * 4 + (lists & 3), lists).astype(f32)
    copies[0].wait()
    for r in range(KEPT):
        s = map_ref[r]
        for a in range(6):
            points = own_ref[a, pl.ds(s, 1), :]
            even_ref[8 * a + r : 8 * a + r + 1, 0:POINTS] = points
            odd_ref[8 * a + r : 8 * a + r + 1, 0:POINTS] = points
    sent_ref[...] = sent
    left = parity("gy") == 1
    for k, ref, base in (
        (jnp.where(left, 0, 2), even_ref, 48),
        (jnp.where(left, 3, 4), even_ref, 56),
        (jnp.where(left, 5, 7), even_ref, 64),
        (jnp.where(left, 2, 0), odd_ref, 48),
        (jnp.where(left, 4, 3), odd_ref, 56),
        (jnp.where(left, 7, 5), odd_ref, 64),
        (6, side_ref, 0),
        (1, side_ref, 8),
    ):
        s = ids_ref[0, 0, k]
        for a in range(6):
            ref[base + a : base + a + 1, 0:POINTS] = own_ref[a, pl.ds(s, 1), :]
        ref[base + 6 : base + 7, 0:128] = sent_ref[pl.ds(k, 1), :]


def pack(ids, moves, source, target, count, own):
    wide = jax.ShapeDtypeStruct((72, WIDE), f32)
    return pl.pallas_call(
        pack_kernel,
        out_shape=(
            jax.ShapeDtypeStruct((8, 128), i32), wide, wide, jax.ShapeDtypeStruct((16, WIDE), f32)
        ),
        in_specs=[pl.BlockSpec(memory_space=pl.ANY)] * 6,
        out_specs=(VMEM,) * 4,
        scratch_shapes=[
            pltpu.VMEM((8, 128), f32),
            pltpu.SMEM(ids.shape, i32),
            pltpu.SMEM(moves.shape, i32),
            pltpu.VMEM(source.shape, i32),
            pltpu.VMEM(target.shape, i32),
            pltpu.SMEM(count.shape, i32),
            pltpu.VMEM(own.shape, f32),
            pltpu.SMEM((CELLS,), i32),
            pltpu.SemaphoreType.DMA((6,)),
        ],
        name="pack",
    )(ids, moves, source, target, count, own)


def join_kernel(sent_ref, side_ref, even_ref, odd_ref, even_out, odd_out):
    up = parity("gx")
    for ref, goes_down in ((even_out, up), (odd_out, 1 - up)):
        side = pl.ds(pl.multiple_of(8 * goes_down, 8), 8)
        place = pl.ds(pl.multiple_of(64 - 16 * goes_down, 8), 8)
        ref[0:48] = sent_ref[0:48]
        ref[48:56] = side_ref[side, :]
        ref[56:104] = even_ref[0:48]
        ref[104:112] = even_ref[place, :]
        ref[112:160] = odd_ref[0:48]
        ref[160:168] = odd_ref[place, :]


def join(sent, side, even, odd):
    wide = jax.ShapeDtypeStruct((168, WIDE), f32)
    return pl.pallas_call(
        join_kernel,
        out_shape=(wide, wide),
        in_specs=[VMEM] * 4,
        out_specs=(VMEM, VMEM),
        compiler_params=pltpu.CompilerParams(vmem_limit_bytes=8 << 20),
        name="join",
    )(sent, side, even, odd)


def own_terms(half, list_ref, own_ref, put, part_ref, source_ref, feature_ref, target_ref):
    leaving = leaving_mask(list_ref)
    part_ref[:, :, WIDE - 128 : WIDE] = jnp.zeros((6, 8, 128), f32)
    for a in range(6):
        part_ref[a, :, 0:POINTS] = own_ref[a, 8 * half : 8 * half + 8, :]
    clear_padding(source_ref, feature_ref, target_ref)
    prepare(lambda a, lanes: part_ref[a, :, lanes], source_ref, feature_ref, target_ref)

    def one_slot(c, carry):
        @pl.when(((leaving >> (c + 8 * half)) & 1) == 0)
        def _():
            put(c, *self_terms(c, source_ref, feature_ref, target_ref))

        return carry

    lax.fori_loop(0, 8, one_slot, 0)


def set_sums(sums_ref, slot, value, add=False):
    rows = pl.ds(pl.multiple_of(slot * 16, 16), 16)
    for col in range(WIDE // 128):
        piece = value[:, 128 * col : 128 * col + 128]
        sums_ref[col, rows, :] = sums_ref[col, rows, :] + piece if add else piece


def open_packet(source, base, quarter_ref, place):
    lane = lax.broadcasted_iota(i32, (8, 256), 1)
    for a in range(6):
        rows = source[base + 8 * a : base + 8 * a + 8]
        for q in range(4):
            turned = rows if q == 0 else pltpu.roll(rows, WIDE - PANEL * q, 1)
            quarter_ref[place, q, 8 * a : 8 * a + 8] = jnp.where(lane < PANEL, turned[:, 0:256], 0.0)


def near_terms(k, place, list_ref, quarter_ref, main_ref, sums_ref, part_ref, near_source, near_feature):
    total = list_ref[k, COUNT_AT]

    def entries(g, which):
        found = []
        for e in which:
            at = jnp.minimum(g * 8 + e, total - 1)
            into = list_ref[k, NEAR + at]
            source = rows_of(near_source, e, 32)
            factors = rows_of(near_feature, e, 48).astype(bf16)
            rows = source.T.astype(bf16)[0:PANEL_ROWS]
            main = [
                main_sums(factors[:, 0:PANEL_ROWS], rows, main_ref[into, :, start:stop])
                for start, stop in NEAR_CHUNKS
            ]
            found.append((into, main))
        for into, main in found:
            set_sums(sums_ref, into, jnp.concatenate(main, 1), True)

    def one_group(g, inner):
        for e in range(8):
            n = g * 8 + e
            live = jnp.where(n < total, 1.0, 0.0)
            panel = list_ref[k, jnp.minimum(n, total - 1)]
            for a in range(6):
                row = quarter_ref[place, panel & 3, pl.ds(8 * a + (panel >> 2), 1), :]
                part_ref[a, e : e + 1, :] = row if a < 3 else row * live
        prepare(lambda a, lanes: part_ref[a, :, lanes], near_source, near_feature)

        @pl.when(g * 8 + 4 < total)
        def _():
            entries(g, range(8))

        @pl.when(g * 8 + 4 >= total)
        def _():
            entries(g, range(4))

        return inner

    lax.fori_loop(0, (total + 7) // 8, one_group, 0)


NEAR_SCRATCH = [
    pltpu.VMEM((8, 128), i32),
    pltpu.SMEM((8, 128), i32),
    pltpu.VMEM((6, 8, 256), f32),
    pltpu.VMEM((2, 256, 128), f32),
    pltpu.VMEM((2, 384, 128), f32),
    pltpu.SemaphoreType.DMA,
]
SELF_SCRATCH = [
    pltpu.VMEM((6, 8, WIDE), f32),
    pltpu.VMEM((5, 256, 128), f32),
    pltpu.VMEM((5, 384, 128), f32),
    pltpu.VMEM((5, 256, 128), f32),
]


def own_kernel(list_ref, own_ref, sums_ref, main_ref, *scratch):
    def put(c, sums, target):
        set_sums(sums_ref, c, sums)
        main_ref[c] = target

    own_terms(0, list_ref, own_ref, put, *scratch)


def own_sums(table, own):
    return pl.pallas_call(
        own_kernel,
        out_shape=(
            jax.ShapeDtypeStruct((5, 8 * 16, 128), f32),
            jax.ShapeDtypeStruct((8, 32, WIDE), bf16),
        ),
        in_specs=[SMEM, VMEM],
        out_specs=(VMEM, VMEM),
        scratch_shapes=SELF_SCRATCH,
        compiler_params=pltpu.CompilerParams(vmem_limit_bytes=24 << 20),
        cost_estimate=pl.CostEstimate(flops=8_000_000_000, bytes_accessed=1 << 20, transcendentals=0),
        name="own",
    )(table, own)


def middle_kernel(
    table_ref, own_ref, first_sums, first_main, even_ref, odd_ref, after_ref, sums_ref, main_ref,
    quarter_ref, number_ref, list_ref, panel_ref, near_source, near_feature, sem, *scratch,
):
    right = parity("gy")
    number_ref[...] = jnp.zeros((8, 128), i32)
    for source, place in ((even_ref, right), (odd_ref, 1 - right)):
        number_ref[pl.ds(3 + place, 1), :] = source[56 + 6 : 56 + 7, 0:128].astype(i32)
        open_packet(source, 0, quarter_ref, place)
    copy = pltpu.make_async_copy(number_ref, list_ref, sem)
    copy.start()
    for col in range(WIDE // 128):
        sums_ref[col, 0:128] = first_sums[col]
    main_ref[0:8] = first_main[...]
    clear_padding(near_source, near_feature)

    def put(c, sums, target):
        set_sums(sums_ref, 8 + c, sums)
        main_ref[8 + c] = target

    own_terms(1, table_ref, own_ref, put, *scratch)
    copy.wait()

    def one_direction(j, carry):
        near_terms(3 + j, j, list_ref, quarter_ref, main_ref, sums_ref, panel_ref, near_source, near_feature)
        return carry

    lax.fori_loop(0, 2, one_direction, 0)


def middle(table, own, first_sums, first_main, even, odd, after):
    return pl.pallas_call(
        middle_kernel,
        out_shape=(
            jax.ShapeDtypeStruct((5, CELLS * 16, 128), f32),
            jax.ShapeDtypeStruct((CELLS, 32, WIDE), bf16),
        ),
        in_specs=[SMEM] + [VMEM] * 5 + [pl.BlockSpec(memory_space=pl.ANY)],
        out_specs=(VMEM, VMEM),
        scratch_shapes=[pltpu.VMEM((2, 4, 48, 256), f32), *NEAR_SCRATCH, *SELF_SCRATCH],
        compiler_params=pltpu.CompilerParams(vmem_limit_bytes=28 << 20),
        cost_estimate=pl.CostEstimate(flops=12_000_000_000, bytes_accessed=1 << 20, transcendentals=0),
        name="middle",
    )(table, own, first_sums, first_main, even, odd, after)


def last_kernel(
    table_ref, own_ref, even_ref, odd_ref, even_side, odd_side, first_sums, main_ref,
    vel_ref, pos_ref,
    quarter_ref, sums_ref, number_ref, list_ref, panel_ref, near_source, near_feature, sem,
    moved_ref, self_source, self_feature, self_target,
):
    right = parity("gy")
    down = 1 - parity("gx")
    for source, base, start, k in (
        (even_ref, None, 56, 3 + right),
        (odd_ref, None, 56, 4 - right),
        (even_side, 0, 48, jnp.where(down == 1, 1, 6)),
        (even_side, 56, 104, jnp.where(down == 1, 2 * right, 5 + 2 * right)),
        (even_side, 112, 160, jnp.where(down == 1, 2 - 2 * right, 7 - 2 * right)),
        (odd_side, 0, 48, jnp.where(down == 1, 6, 1)),
        (odd_side, 56, 104, jnp.where(down == 1, 5 + 2 * right, 2 * right)),
        (odd_side, 112, 160, jnp.where(down == 1, 7 - 2 * right, 2 - 2 * right)),
    ):
        block = source[start : start + 8]
        number_ref[pl.ds(k, 1), :] = block[6:7, 0:128].astype(i32)
        for a in range(6):
            moved_ref[a, pl.ds(k, 1), :] = block[a : a + 1]
        if base is not None:
            open_packet(source, base, quarter_ref, k)
    copy = pltpu.make_async_copy(number_ref, list_ref, sem)
    copy.start()
    for col in range(WIDE // 128):
        sums_ref[col, 0 : CELLS * 16] = first_sums[col]
    clear_padding(near_source, near_feature)
    clear_padding(self_source, self_feature, self_target)
    prepare(lambda a, lanes: moved_ref[a, :, lanes], self_source, self_feature, self_target)
    leaving = leaving_mask(table_ref)
    copy.wait()

    def one_move(k, carry):
        @pl.when(list_ref[k, MOVES_AT] > 0)
        def _():
            set_sums(sums_ref, CELLS + k, self_terms(k, self_source, self_feature, self_target)[0])

        return carry

    lax.fori_loop(0, 8, one_move, 0)

    def one_direction(j, carry):
        k = jnp.where(j < 3, j, j + 2)
        near_terms(k, k, list_ref, quarter_ref, main_ref, sums_ref, panel_ref, near_source, near_feature)
        return carry

    lax.fori_loop(0, 6, one_direction, 0)

    row = lax.broadcasted_iota(i32, (8, 128), 0)
    for h in range(3):
        alive = jnp.zeros((8, 128), i32)
        for c in range(8):
            here = 1 - ((leaving >> (8 * h + c)) & 1) if h < 2 else jnp.where(list_ref[c, MOVES_AT] > 0, 1, 0)
            alive = jnp.where(row == c, here, alive)
        for start in range(0, WIDE, 128):
            stop = min(start + 128, POINTS)
            lanes = slice(start, stop)
            living = alive[:, 0 : stop - start] > 0
            x = [own_ref[a, 8 * h : 8 * h + 8, lanes] if h < 2 else moved_ref[a, :, lanes] for a in range(3)]
            sums = [sums_ref[start // 128, pl.ds(128 * h + f, 8, stride=16), :][:, 0 : stop - start] for f in range(15)]
            p = sums[0:3]
            r = [sums[3 + 3 * a : 6 + 3 * a] for a in range(3)]
            norm = x[0] * x[0] + x[1] * x[1] + x[2] * x[2] + 2.0 * reg_square
            inner = x[0] * p[0] + x[1] * p[1] + x[2] * p[2] - (r[0][0] + r[1][1] + r[2][2])
            for b in range(3):
                u = norm * p[b] + x[b] * inner + sums[12 + b]
                for a in range(3):
                    u = u - x[a] * (2.0 * r[a][b] + r[b][a])
                u = u * kernel_scale
                vel_ref[b, 8 * h : 8 * h + 8, lanes] = jnp.where(living, u, 0.0)
                pos_ref[b, 8 * h : 8 * h + 8, lanes] = jnp.where(living, x[b] + time_step * u, 0.0)


def last(table, own, even, odd, even_side, odd_side, sums, main):
    out = jax.ShapeDtypeStruct((3, CELLS + 8, POINTS), f32)
    return pl.pallas_call(
        last_kernel,
        out_shape=(out, out),
        in_specs=[SMEM] + [VMEM] * 7,
        out_specs=(VMEM, VMEM),
        scratch_shapes=[
            pltpu.VMEM((8, 4, 48, 256), f32),
            pltpu.VMEM((5, (CELLS + 8) * 16, 128), f32),
            *NEAR_SCRATCH,
            *SELF_SCRATCH,
        ],
        compiler_params=pltpu.CompilerParams(vmem_limit_bytes=32 << 20),
        cost_estimate=pl.CostEstimate(flops=40_000_000_000, bytes_accessed=1 << 20, transcendentals=0),
        name="last",
    )(table, own, even, odd, even_side, odd_side, sums, main)


def on_device(surface, mig_ids, mig_count, near_source, near_target, near_count):
    own = surface[:, 0, 0]
    ids = mig_ids[:, :, :, 0]
    table, to_even, to_odd, side = pack(ids, mig_count, near_source, near_target, near_count, own)
    even = swap(to_even, "gy", 0)
    odd = swap(to_odd, "gy", 1)
    first_sums, first_main = own_sums(table, own)
    side_even, side_odd = join(to_even, side, even, odd)
    even_side = swap(side_even, "gx", 0)
    odd_side = swap(side_odd, "gx", 1)
    sums, main = middle(table, own, first_sums, first_main, even, odd, side_even)
    vel, pos = last(table, own, even, odd, even_side, odd_side, sums, main)
    return vel[:, None, None], pos[:, None, None]


def solution(mesh):
    placed = (
        P(None, "gx", "gy", None, None),
        P("gx", "gy", None, None),
        P("gx", "gy", None),
        P("gx", "gy", None, None),
        P("gx", "gy", None, None),
        P("gx", "gy", None),
    )
    return jax.shard_map(
        on_device,
        mesh=mesh,
        in_specs=placed,
        out_specs=(P(None, "gx", "gy", None, None), P(None, "gx", "gy", None, None)),
        check_vma=False,
    )
```

```python
import functools

import jax
import jax.numpy as jnp
from jax import lax
from jax.experimental import pallas as pl
from jax.experimental.pallas import tpu as pltpu
from jax.sharding import PartitionSpec as P

neighbours = ((-1, -1), (-1, 0), (-1, 1), (0, -1), (0, 1), (1, -1), (1, 0), (1, 1))
reg_square = 0.09
kernel_scale = 1.0 / (8.0 * 3.141592653589793)
time_step = 0.1

f32 = jnp.float32
bf16 = jnp.bfloat16
i32 = jnp.int32

CELLS = 16
POINTS = 544
WIDE = 640
PANEL = 136
PANEL_ROWS = 144
KEPT = 8
NEAR = 16
COUNT_AT = 2 * NEAR
MOVES_AT = 2 * NEAR + 1
IDS_AT = 2 * NEAR + 2
SELF_CHUNKS = ((0, 640),)
NEAR_CHUNKS = ((0, 256), (256, 512), (512, 640))

VMEM = pl.BlockSpec(memory_space=pltpu.VMEM)
SMEM = pl.BlockSpec(memory_space=pltpu.SMEM)


def from_behind(value, axis, by):
    size = lax.axis_size(axis)
    return lax.ppermute(value, axis, [(i, (i + by) % size) for i in range(size)])


def split3(value):
    high = value.astype(bf16).astype(f32)
    rest = value - high
    middle = rest.astype(bf16).astype(f32)
    return high, middle, rest - middle


def prepare(part, source_ref, feature_ref, target_ref=None):
    for col in range(source_ref.shape[0]):
        lanes = slice(128 * col, 128 * col + 128)
        pos = [part(a, lanes) for a in range(3)]
        den = [part(3 + a, lanes) for a in range(3)]
        norm = pos[0] * pos[0] + pos[1] * pos[1] + pos[2] * pos[2]
        dot = pos[0] * den[0] + pos[1] * den[1] + pos[2] * den[2]
        pieces = [split3(p) for p in pos]
        one = jnp.ones_like(norm)
        rows = [pieces[a][p] for p in (0, 1, 0, 1, 2, 0) for a in range(3)]
        rows += [*split3(norm + reg_square), one, one, one]
        for i, row in enumerate(rows):
            source_ref[col, 8 * i : 8 * i + 8, :] = row
        if target_ref is not None:
            rows = [-2.0 * pieces[a][p] for p in (0, 0, 1, 1, 0, 2) for a in range(3)]
            rows += [one, one, one, *split3(norm)]
            for i, row in enumerate(rows):
                target_ref[col, 8 * i : 8 * i + 8, :] = row
        found = [*den]
        found += [pos[a] * den[b] for a in range(3) for b in range(3)]
        found += [norm * den[b] + dot * pos[b] for b in range(3)]
        for f, value in enumerate(found):
            for p, piece in enumerate(split3(value)):
                row = 8 * (16 * p + f)
                feature_ref[col, row : row + 8, :] = piece


def clear_padding(source_ref, feature_ref, target_ref=None):
    for col in range(source_ref.shape[0]):
        for ref in (source_ref, target_ref):
            if ref is not None:
                ref[col, 8 * 24 : 8 * 32, :] = jnp.zeros((64, 128), f32)
        for p in range(3):
            row = 8 * (16 * p + 15)
            feature_ref[col, row : row + 8, :] = jnp.zeros((8, 128), f32)


def rows_of(ref, c, rows):
    cols = range(ref.shape[0])
    return jnp.concatenate([ref[col, pl.ds(c, rows, stride=8), :] for col in cols], 1)


def weights(shifted):
    inverse = lax.rsqrt(shifted)
    weight = inverse * inverse * inverse
    high = weight.astype(bf16)
    return high, (weight - high.astype(f32)).astype(bf16)


def main_sums(factors, source, target):
    high, low = weights(jnp.dot(source, target, preferred_element_type=f32))
    first = jnp.dot(factors, high, preferred_element_type=f32)
    second = jnp.dot(factors[0:32], low, preferred_element_type=f32)
    return (first[0:16] + second[0:16]) + ((first[16:32] + second[16:32]) + first[32:48])


def self_terms(c, source_ref, feature_ref, target_ref):
    source = rows_of(source_ref, c, 32)
    factors = rows_of(feature_ref, c, 48).astype(bf16)
    target = rows_of(target_ref, c, 32).astype(bf16)
    rows = source.T.astype(bf16)[0:POINTS]
    found = [
        main_sums(factors[:, 0:POINTS], rows, target[:, start:stop]) for start, stop in SELF_CHUNKS
    ]
    return jnp.concatenate(found, 1), target


def leaving_mask(list_ref):
    mask = jnp.int32(0)
    for k in range(8):
        bit = jnp.int32(1) << list_ref[k, IDS_AT]
        mask = mask | jnp.where(list_ref[k, MOVES_AT] > 0, bit, jnp.int32(0))
    return mask


def pack_kernel(
    ids_hbm, moves_hbm, source_hbm, target_hbm, count_hbm, own_hbm,
    table_ref, low_ref, high_ref, side_ref,
    sent_ref, ids_ref, moves_ref, source_ref, target_ref, count_ref, own_ref, map_ref, sems,
):
    copies = [
        pltpu.make_async_copy(here, there, sems.at[n])
        for n, (here, there) in enumerate(
            (
                (own_hbm, own_ref),
                (ids_hbm, ids_ref),
                (moves_hbm, moves_ref),
                (count_hbm, count_ref),
                (source_hbm, source_ref),
                (target_hbm, target_ref),
            )
        )
    ]
    for copy in copies:
        copy.start()
    for ref in (low_ref, high_ref, side_ref):
        ref[...] = jnp.zeros(ref.shape, f32)
    table_ref[...] = jnp.zeros((8, 128), i32)
    for copy in copies[1:]:
        copy.wait()
    table_ref[:, 0:NEAR] = source_ref[0, 0]
    table_ref[:, NEAR : 2 * NEAR] = target_ref[0, 0]
    lists = table_ref[...]
    row = lax.broadcasted_iota(i32, (8, 128), 0)
    lane = lax.broadcasted_iota(i32, (8, 128), 1)
    used = jnp.int32(0)
    for k in range(8):
        used = used | (jnp.int32(1) << ids_ref[0, 0, k])
        for column, value in (
            (COUNT_AT, count_ref[0, 0, k]),
            (MOVES_AT, moves_ref[0, 0, k]),
            (IDS_AT, ids_ref[0, 0, k]),
        ):
            lists = jnp.where((row == k) & (lane == column), value, lists)
    table_ref[...] = lists
    rank = jnp.int32(0)
    slot = lists >> 2
    ranked = jnp.zeros((8, 128), i32)
    for s in range(CELLS):
        map_ref[s] = jnp.int32(0)
    for s in range(CELLS):
        keep = ((used >> s) & 1) == 0
        ranked = jnp.where(slot == s, rank, ranked)
        map_ref[jnp.where(keep, rank, CELLS - 1)] = jnp.int32(s)
        rank = jnp.where(keep & (rank < KEPT - 1), rank + 1, rank)
    sent = jnp.where(lane < NEAR, ranked * 4 + (lists & 3), lists).astype(f32)
    copies[0].wait()
    for r in range(KEPT):
        s = map_ref[r]
        for a in range(6):
            points = own_ref[a, pl.ds(s, 1), :]
            low_ref[8 * a + r : 8 * a + r + 1, 0:POINTS] = points
            high_ref[8 * a + r : 8 * a + r + 1, 0:POINTS] = points
    sent_ref[...] = sent
    for k, ref, base in (
        (2, low_ref, 48),
        (4, low_ref, 56),
        (7, low_ref, 64),
        (0, high_ref, 48),
        (3, high_ref, 56),
        (5, high_ref, 64),
        (6, side_ref, 0),
        (1, side_ref, 8),
    ):
        s = ids_ref[0, 0, k]
        for a in range(6):
            ref[base + a : base + a + 1, 0:POINTS] = own_ref[a, pl.ds(s, 1), :]
        ref[base + 6 : base + 7, 0:128] = sent_ref[k : k + 1, :]


def pack(ids, moves, source, target, count, own):
    wide = jax.ShapeDtypeStruct((72, WIDE), f32)
    return pl.pallas_call(
        pack_kernel,
        out_shape=(
            jax.ShapeDtypeStruct((8, 128), i32), wide, wide, jax.ShapeDtypeStruct((16, WIDE), f32)
        ),
        in_specs=[pl.BlockSpec(memory_space=pl.ANY)] * 6,
        out_specs=(VMEM,) * 4,
        scratch_shapes=[
            pltpu.VMEM((8, 128), f32),
            pltpu.SMEM(ids.shape, i32),
            pltpu.SMEM(moves.shape, i32),
            pltpu.VMEM(source.shape, i32),
            pltpu.VMEM(target.shape, i32),
            pltpu.SMEM(count.shape, i32),
            pltpu.VMEM(own.shape, f32),
            pltpu.SMEM((CELLS,), i32),
            pltpu.SemaphoreType.DMA((6,)),
        ],
        name="pack",
    )(ids, moves, source, target, count, own)


def join_kernel(sent_ref, side_ref, low_ref, high_ref, up_out, down_out):
    for ref, goes_down in ((up_out, 0), (down_out, 1)):
        side = slice(8 * goes_down, 8 * goes_down + 8)
        place = slice(64 - 16 * goes_down, 72 - 16 * goes_down)
        ref[0:48] = sent_ref[0:48]
        ref[48:56] = side_ref[side, :]
        ref[56:104] = low_ref[0:48]
        ref[104:112] = low_ref[place, :]
        ref[112:160] = high_ref[0:48]
        ref[160:168] = high_ref[place, :]


def join(sent, side, low, high):
    wide = jax.ShapeDtypeStruct((168, WIDE), f32)
    return pl.pallas_call(
        join_kernel,
        out_shape=(wide, wide),
        in_specs=[VMEM] * 4,
        out_specs=(VMEM, VMEM),
        compiler_params=pltpu.CompilerParams(vmem_limit_bytes=8 << 20),
        name="join",
    )(sent, side, low, high)


def own_terms(half, list_ref, own_ref, put, part_ref, source_ref, feature_ref, target_ref):
    leaving = leaving_mask(list_ref)
    part_ref[:, :, WIDE - 128 : WIDE] = jnp.zeros((6, 8, 128), f32)
    for a in range(6):
        part_ref[a, :, 0:POINTS] = own_ref[a, 8 * half : 8 * half + 8, :]
    clear_padding(source_ref, feature_ref, target_ref)
    prepare(lambda a, lanes: part_ref[a, :, lanes], source_ref, feature_ref, target_ref)

    def one_slot(c, carry):
        @pl.when(((leaving >> (c + 8 * half)) & 1) == 0)
        def _():
            put(c, *self_terms(c, source_ref, feature_ref, target_ref))

        return carry

    lax.fori_loop(0, 8, one_slot, 0)


def set_sums(sums_ref, slot, value, add=False):
    rows = pl.ds(pl.multiple_of(slot * 16, 16), 16)
    for col in range(WIDE // 128):
        piece = value[:, 128 * col : 128 * col + 128]
        sums_ref[col, rows, :] = sums_ref[col, rows, :] + piece if add else piece


def open_packet(source, base, quarter_ref, place):
    lane = lax.broadcasted_iota(i32, (8, 256), 1)
    for a in range(6):
        rows = source[base + 8 * a : base + 8 * a + 8]
        for q in range(4):
            turned = rows if q == 0 else pltpu.roll(rows, WIDE - PANEL * q, 1)
            quarter_ref[place, q, 8 * a : 8 * a + 8] = jnp.where(lane < PANEL, turned[:, 0:256], 0.0)


def near_terms(k, place, list_ref, quarter_ref, main_ref, sums_ref, part_ref, near_source, near_feature):
    total = list_ref[k, COUNT_AT]

    def entries(g, which):
        found = []
        for e in which:
            at = jnp.minimum(g * 8 + e, total - 1)
            into = list_ref[k, NEAR + at]
            source = rows_of(near_source, e, 32)
            factors = rows_of(near_feature, e, 48).astype(bf16)
            rows = source.T.astype(bf16)[0:PANEL_ROWS]
            main = [
                main_sums(factors[:, 0:PANEL_ROWS], rows, main_ref[into, :, start:stop])
                for start, stop in NEAR_CHUNKS
            ]
            found.append((into, main))
        for into, main in found:
            set_sums(sums_ref, into, jnp.concatenate(main, 1), True)

    def one_group(g, inner):
        for e in range(8):
            n = g * 8 + e
            live = jnp.where(n < total, 1.0, 0.0)
            panel = list_ref[k, jnp.minimum(n, total - 1)]
            for a in range(6):
                row = quarter_ref[place, panel & 3, pl.ds(8 * a + (panel >> 2), 1), :]
                part_ref[a, e : e + 1, :] = row if a < 3 else row * live
        prepare(lambda a, lanes: part_ref[a, :, lanes], near_source, near_feature)

        @pl.when(g * 8 + 4 < total)
        def _():
            entries(g, range(8))

        @pl.when(g * 8 + 4 >= total)
        def _():
            entries(g, range(4))

        return inner

    lax.fori_loop(0, (total + 7) // 8, one_group, 0)


NEAR_SCRATCH = [
    pltpu.VMEM((8, 128), i32),
    pltpu.SMEM((8, 128), i32),
    pltpu.VMEM((6, 8, 256), f32),
    pltpu.VMEM((2, 256, 128), f32),
    pltpu.VMEM((2, 384, 128), f32),
    pltpu.SemaphoreType.DMA,
]
SELF_SCRATCH = [
    pltpu.VMEM((6, 8, WIDE), f32),
    pltpu.VMEM((5, 256, 128), f32),
    pltpu.VMEM((5, 384, 128), f32),
    pltpu.VMEM((5, 256, 128), f32),
]


def own_kernel(list_ref, own_ref, sums_ref, main_ref, *scratch):
    def put(c, sums, target):
        set_sums(sums_ref, c, sums)
        main_ref[c] = target

    own_terms(0, list_ref, own_ref, put, *scratch)


def own_sums(table, own):
    return pl.pallas_call(
        own_kernel,
        out_shape=(
            jax.ShapeDtypeStruct((5, 8 * 16, 128), f32),
            jax.ShapeDtypeStruct((8, 32, WIDE), bf16),
        ),
        in_specs=[SMEM, VMEM],
        out_specs=(VMEM, VMEM),
        scratch_shapes=SELF_SCRATCH,
        compiler_params=pltpu.CompilerParams(vmem_limit_bytes=24 << 20),
        cost_estimate=pl.CostEstimate(flops=8_000_000_000, bytes_accessed=1 << 20, transcendentals=0),
        name="own",
    )(table, own)


def middle_kernel(
    table_ref, own_ref, first_sums, first_main, low_ref, high_ref, after_ref, sums_ref, main_ref,
    quarter_ref, number_ref, list_ref, panel_ref, near_source, near_feature, sem, *scratch,
):
    number_ref[...] = jnp.zeros((8, 128), i32)
    for source, place in ((low_ref, 1), (high_ref, 0)):
        number_ref[3 + place : 4 + place, :] = source[56 + 6 : 56 + 7, 0:128].astype(i32)
        open_packet(source, 0, quarter_ref, place)
    copy = pltpu.make_async_copy(number_ref, list_ref, sem)
    copy.start()
    for col in range(WIDE // 128):
        sums_ref[col, 0:128] = first_sums[col]
    main_ref[0:8] = first_main[...]
    clear_padding(near_source, near_feature)

    def put(c, sums, target):
        set_sums(sums_ref, 8 + c, sums)
        main_ref[8 + c] = target

    own_terms(1, table_ref, own_ref, put, *scratch)
    copy.wait()

    def one_direction(j, carry):
        near_terms(3 + j, j, list_ref, quarter_ref, main_ref, sums_ref, panel_ref, near_source, near_feature)
        return carry

    lax.fori_loop(0, 2, one_direction, 0)


def middle(table, own, first_sums, first_main, low, high, after):
    return pl.pallas_call(
        middle_kernel,
        out_shape=(
            jax.ShapeDtypeStruct((5, CELLS * 16, 128), f32),
            jax.ShapeDtypeStruct((CELLS, 32, WIDE), bf16),
        ),
        in_specs=[SMEM] + [VMEM] * 5 + [pl.BlockSpec(memory_space=pl.ANY)],
        out_specs=(VMEM, VMEM),
        scratch_shapes=[pltpu.VMEM((2, 4, 48, 256), f32), *NEAR_SCRATCH, *SELF_SCRATCH],
        compiler_params=pltpu.CompilerParams(vmem_limit_bytes=28 << 20),
        cost_estimate=pl.CostEstimate(flops=12_000_000_000, bytes_accessed=1 << 20, transcendentals=0),
        name="middle",
    )(table, own, first_sums, first_main, low, high, after)


def last_kernel(
    table_ref, own_ref, low_ref, high_ref, up, down, first_sums, main_ref,
    vel_ref, pos_ref,
    quarter_ref, sums_ref, number_ref, list_ref, panel_ref, near_source, near_feature, sem,
    moved_ref, self_source, self_feature, self_target,
):
    for source, base, start, k in (
        (low_ref, None, 56, 4),
        (high_ref, None, 56, 3),
        (up, 0, 48, 6),
        (up, 56, 104, 7),
        (up, 112, 160, 5),
        (down, 0, 48, 1),
        (down, 56, 104, 2),
        (down, 112, 160, 0),
    ):
        block = source[start : start + 8]
        number_ref[k : k + 1, :] = block[6:7, 0:128].astype(i32)
        for a in range(6):
            moved_ref[a, k : k + 1, :] = block[a : a + 1]
        if base is not None:
            open_packet(source, base, quarter_ref, k)
    copy = pltpu.make_async_copy(number_ref, list_ref, sem)
    copy.start()
    for col in range(WIDE // 128):
        sums_ref[col, 0 : CELLS * 16] = first_sums[col]
    clear_padding(near_source, near_feature)
    clear_padding(self_source, self_feature, self_target)
    prepare(lambda a, lanes: moved_ref[a, :, lanes], self_source, self_feature, self_target)
    leaving = leaving_mask(table_ref)
    copy.wait()

    def one_move(k, carry):
        @pl.when(list_ref[k, MOVES_AT] > 0)
        def _():
            set_sums(sums_ref, CELLS + k, self_terms(k, self_source, self_feature, self_target)[0])

        return carry

    lax.fori_loop(0, 8, one_move, 0)

    def one_direction(j, carry):
        k = jnp.where(j < 3, j, j + 2)
        near_terms(k, k, list_ref, quarter_ref, main_ref, sums_ref, panel_ref, near_source, near_feature)
        return carry

    lax.fori_loop(0, 6, one_direction, 0)

    row = lax.broadcasted_iota(i32, (8, 128), 0)
    for h in range(3):
        alive = jnp.zeros((8, 128), i32)
        for c in range(8):
            here = 1 - ((leaving >> (8 * h + c)) & 1) if h < 2 else jnp.where(list_ref[c, MOVES_AT] > 0, 1, 0)
            alive = jnp.where(row == c, here, alive)
        for start in range(0, WIDE, 128):
            stop = min(start + 128, POINTS)
            lanes = slice(start, stop)
            living = alive[:, 0 : stop - start] > 0
            x = [own_ref[a, 8 * h : 8 * h + 8, lanes] if h < 2 else moved_ref[a, :, lanes] for a in range(3)]
            sums = [sums_ref[start // 128, pl.ds(128 * h + f, 8, stride=16), :][:, 0 : stop - start] for f in range(15)]
            p = sums[0:3]
            r = [sums[3 + 3 * a : 6 + 3 * a] for a in range(3)]
            norm = x[0] * x[0] + x[1] * x[1] + x[2] * x[2] + 2.0 * reg_square
            inner = x[0] * p[0] + x[1] * p[1] + x[2] * p[2] - (r[0][0] + r[1][1] + r[2][2])
            for b in range(3):
                u = norm * p[b] + x[b] * inner + sums[12 + b]
                for a in range(3):
                    u = u - x[a] * (2.0 * r[a][b] + r[b][a])
                u = u * kernel_scale
                vel_ref[b, 8 * h : 8 * h + 8, lanes] = jnp.where(living, u, 0.0)
                pos_ref[b, 8 * h : 8 * h + 8, lanes] = jnp.where(living, x[b] + time_step * u, 0.0)


def last(table, own, low, high, up, down, sums, main):
    out = jax.ShapeDtypeStruct((3, CELLS + 8, POINTS), f32)
    return pl.pallas_call(
        last_kernel,
        out_shape=(out, out),
        in_specs=[SMEM] + [VMEM] * 7,
        out_specs=(VMEM, VMEM),
        scratch_shapes=[
            pltpu.VMEM((8, 4, 48, 256), f32),
            pltpu.VMEM((5, (CELLS + 8) * 16, 128), f32),
            *NEAR_SCRATCH,
            *SELF_SCRATCH,
        ],
        compiler_params=pltpu.CompilerParams(vmem_limit_bytes=32 << 20),
        cost_estimate=pl.CostEstimate(flops=40_000_000_000, bytes_accessed=1 << 20, transcendentals=0),
        name="last",
    )(table, own, low, high, up, down, sums, main)


def on_device(surface, mig_ids, mig_count, near_source, near_target, near_count):
    own = surface[:, 0, 0]
    ids = mig_ids[:, :, :, 0]
    table, to_right, to_left, side = pack(ids, mig_count, near_source, near_target, near_count, own)
    low = from_behind(to_right, "gy", 1)
    high = from_behind(to_left, "gy", -1)
    first_sums, first_main = own_sums(table, own)
    to_up, to_down = join(to_right, side, low, high)
    up = from_behind(to_up, "gx", 1)
    down = from_behind(to_down, "gx", -1)
    sums, main = middle(table, own, first_sums, first_main, low, high, to_up)
    vel, pos = last(table, own, low, high, up, down, sums, main)
    return vel[:, None, None], pos[:, None, None]


def solution(mesh):
    placed = (
        P(None, "gx", "gy", None, None),
        P("gx", "gy", None, None),
        P("gx", "gy", None),
        P("gx", "gy", None, None),
        P("gx", "gy", None, None),
        P("gx", "gy", None),
    )
    return jax.shard_map(
        on_device,
        mesh=mesh,
        in_specs=placed,
        out_specs=(P(None, "gx", "gy", None, None), P(None, "gx", "gy", None, None)),
        check_vma=False,
    )
```
